32 devices in a mesh: dp: 4 (over z), expert: 8 (over y, x, core).
Axes of the slice: x: 2, y: 2, z: 4, core: 2. Of those that a mesh axis runs over, the one named last changes fastest.
Arguments:
- tokens: bfloat16 [4096, 4096], P(('dp', 'expert')), may hold values from -6 to 6
- expert_ids: int32 [4096, 2], P(('dp', 'expert')), may hold values from 0 to 7, all different within a row; in each aligned block of 128 rows (0 to 127, 128 to 255, ...) at most 36 rows name the same one
- router_probs: float32 [4096, 2], P(('dp', 'expert')), may hold values from 0.1 to 1
- w_gate: bfloat16 [8, 1024, 4096], P('expert', 'dp'), may hold values from -0.09375 to 0.09375
- w_up: bfloat16 [8, 1024, 4096], P('expert', 'dp'), may hold values from -0.09375 to 0.09375
- w_down: bfloat16 [8, 1024, 4096], P('expert', 'dp'), may hold values from -0.1875 to 0.1875
- out_grad: bfloat16 [4096, 4096], P(('dp', 'expert')), may hold values from -6 to 6
Outputs:
- mixed: bfloat16 [4096, 4096], P(('dp', 'expert'))
- input_grad: bfloat16 [4096, 4096], P(('dp', 'expert'))
- prob_grad: float32 [4096, 2], P(('dp', 'expert'))
- grad_gate: bfloat16 [8, 1024, 4096], P('expert', 'dp')
- grad_up: bfloat16 [8, 1024, 4096], P('expert', 'dp')
- grad_down: bfloat16 [8, 1024, 4096], P('expert', 'dp')
The draws below stay inside these ranges and needn't reach their ends.
Inputs may be any that keep to these rules, and one draw needn't show every extreme that they name: `expert_ids`: each row names 2 different experts. Among the rows of one device no expert is named more than 36 times, a bound that some block reaches.
All inputs are finite; a program needn't handle non-finite values.
Results may differ from the reference program's by a relative error of at most 0.018.
Values may be sent and summed in bfloat16 or wider, within the bound.
A program may use at most 192 MiB of HBM per device.

```python
import math
import jax
import jax.numpy as jnp
import numpy as np
from jax import lax

D = 4096
FFW = 1024
TOPK = 2
TOK_DEV = 128
EXPERTS = 8
MOST = 36
TOKENS = 4096
N_DP = 4
N_EXPERT = 8


def steps_of(own_key, dims, split, low, top_value):
    level, own = 1.0, jax.random.fold_in(own_key, 6)
    for axis_at, shards_of in split:
        steps = jnp.exp(jax.random.uniform(jax.random.fold_in(own, axis_at), (shards_of,), jnp.float32, low / len(split), top_value / len(split)))
        level = level * jnp.repeat(steps, dims[axis_at] // shards_of).reshape([-1 if axis == axis_at else 1 for axis in range(len(dims))])
    return level


def assign_block(key, own, number, rows, count, top, most, skew):
    ranking = jax.random.permutation(key, count)
    packed, common = load_shares(count, rows * top, most, skew, True), load_shares(count, rows * top, most, skew, False)
    places = jnp.arange(count)

    def named(lengths, turn):
        used = int((lengths > 0).sum())
        fixed = max(1, used // 4)
        passed = fixed + (places - fixed + turn * (used - fixed)) % max(1, count - fixed)
        return jnp.zeros((count,), jnp.int32).at[ranking[jnp.where(places < fixed, places, passed)]].set(jnp.asarray(lengths, jnp.int32))

    lengths = jnp.where(number % 4 == 0, named(packed, number // 4), named(common, number - number // 4 - 1))
    mixed = jax.random.permutation(jax.random.fold_in(own, 3), count)
    donor, receiver = mixed[0:count // 2 * 2:2], mixed[1:count // 2 * 2:2]
    margin = jnp.minimum(lengths[donor] - 1, most - lengths[receiver]) // 2
    margin = jnp.where((donor == ranking[0]) | (receiver == ranking[0]) | (lengths[receiver] == 0), 0, jnp.maximum(margin, 0))
    passed = jax.random.randint(jax.random.fold_in(own, 4), (count // 2,), 0, 1 << 20) % (margin + 1)
    lengths = lengths.at[donor].add(-passed).at[receiver].add(passed)
    items = jnp.searchsorted(jnp.cumsum(lengths), jnp.arange(rows * top), side="right").astype(jnp.int32)
    listing = items.reshape(top, rows).T
    listing = listing[jax.random.permutation(jax.random.fold_in(own, 1), rows)]
    turn = jax.random.randint(jax.random.fold_in(own, 2), (rows, 1), 0, top)
    return jnp.take_along_axis(listing, (jnp.arange(top)[None, :] + turn) % top, axis=1)


def load_shares(count, total, limit, lean, full):
    loads = [(1 << 20) // math.isqrt(rank ** lean) + 1 for rank in range(1, count + 1)]
    largest = limit if full else min(limit, max(-(-total // count), total * loads[0] // sum(loads)))
    least = 1 if total - largest >= count - 1 else 0
    counts, spare = [largest] + [least] * (count - 1), total - largest - least * (count - 1)
    while spare > 0:
        movable = [i for i in range(1, count) if counts[i] < largest] or [i for i in range(1, count) if counts[i] < limit]
        mass, remaining = sum([loads[i] for i in movable]), spare
        for i in movable:
            extra = min(limit - counts[i], max(1, remaining * loads[i] // mass), spare)
            counts[i] = counts[i] + extra
            spare = spare - extra
    return np.array(counts)


def bell_draw(key, dims, width, limit, pieces=(), kind=jnp.bfloat16):
    drawn = width * jax.random.normal(key, dims, jnp.float32)
    if pieces:
        drawn = drawn * steps_of(key, dims, pieces, -0.22, 0.18)
    return jnp.clip(drawn, -limit, limit).astype(kind)


def setup_inputs(seed: int = 0) -> dict:
    splits = jax.random.split(jax.random.key(seed), 8)
    tokens = bell_draw(splits[0], (TOKENS, D), 1.0, 6.0, ((0, 32),))
    expert_ids_keys = jax.random.split(jax.random.fold_in(splits[1], 1), TOKENS // TOK_DEV)
    expert_ids_turns = jax.random.permutation(jax.random.fold_in(splits[1], 3), TOKENS // TOK_DEV)
    expert_ids = jax.vmap(lambda own, number: assign_block(jax.random.fold_in(splits[1], 2), own, number, TOK_DEV, EXPERTS, TOPK, MOST, 2))(expert_ids_keys, expert_ids_turns).reshape((TOKENS, TOPK))
    router_probs = jnp.clip(0.1 + 0.9 * jax.random.uniform(splits[2], (TOKENS, TOPK), jnp.float32) ** steps_of(splits[2], (TOKENS, TOPK), ((0, 32),), -0.2, 0.2), 0.1, 1.0)
    w_gate = bell_draw(splits[3], (EXPERTS, FFW, D), D ** -0.5, 0.09375, ((0, 8), (1, 4)))
    w_up = bell_draw(splits[4], (EXPERTS, FFW, D), D ** -0.5, 0.09375, ((0, 8), (1, 4)))
    w_down = bell_draw(splits[5], (EXPERTS, FFW, D), FFW ** -0.5, 0.1875, ((0, 8), (1, 4)))
    out_grad = bell_draw(splits[6], (TOKENS, D), 1.0, 6.0, ((0, 32),))
    return dict(tokens=tokens, expert_ids=expert_ids, router_probs=router_probs, w_gate=w_gate, w_up=w_up, w_down=w_down, out_grad=out_grad)


def expert_pass(tok_slots, grad_slots, gate_w, up_w, down_w):
    gate_proj = jnp.dot(tok_slots, gate_w.T, preferred_element_type=jnp.float32)
    up_proj = jnp.dot(tok_slots, up_w.T, preferred_element_type=jnp.float32)
    sigmoid_gate = jax.nn.sigmoid(gate_proj)
    activated = gate_proj * sigmoid_gate
    hidden = (activated * up_proj).astype(jnp.bfloat16)
    d_hidden = jnp.dot(grad_slots, down_w.T, preferred_element_type=jnp.float32)
    d_gate = (d_hidden * up_proj * sigmoid_gate * (1.0 + gate_proj * (1.0 - sigmoid_gate))).astype(jnp.bfloat16)
    d_up = (d_hidden * activated).astype(jnp.bfloat16)
    quarter_width = FFW // N_DP
    out_sum = jnp.zeros((tok_slots.shape[0], D), jnp.float32)
    back_sum = jnp.zeros((tok_slots.shape[0], D), jnp.float32)
    for part_index in range(N_DP):
        lower = part_index * quarter_width
        upper = lower + quarter_width
        part_out = jnp.dot(hidden[:, lower:upper], down_w[lower:upper], preferred_element_type=jnp.float32)
        part_out = lax.optimization_barrier(part_out.astype(jnp.bfloat16))
        out_sum = out_sum + part_out.astype(jnp.float32)
        part_back = jnp.dot(d_gate[:, lower:upper], gate_w[lower:upper], preferred_element_type=jnp.float32)
        part_back = part_back + jnp.dot(d_up[:, lower:upper], up_w[lower:upper], preferred_element_type=jnp.float32)
        part_back = lax.optimization_barrier(part_back.astype(jnp.bfloat16))
        back_sum = back_sum + part_back.astype(jnp.float32)
    grad_down_e = jnp.dot(hidden.T, grad_slots, preferred_element_type=jnp.float32).astype(jnp.bfloat16)
    grad_gate_e = jnp.dot(d_gate.T, tok_slots, preferred_element_type=jnp.float32).astype(jnp.bfloat16)
    grad_up_e = jnp.dot(d_up.T, tok_slots, preferred_element_type=jnp.float32).astype(jnp.bfloat16)
    return out_sum.astype(jnp.bfloat16), back_sum.astype(jnp.bfloat16), grad_gate_e, grad_up_e, grad_down_e


def reference(tokens, expert_ids, router_probs, w_gate, w_up, w_down, out_grad):
    devices = N_DP * N_EXPERT
    per_device = TOK_DEV * TOPK
    id_table = expert_ids.reshape(devices, per_device).astype(jnp.int32)
    onehot = (id_table[:, :, None] == jnp.arange(EXPERTS, dtype=jnp.int32)[None, None, :]).astype(jnp.int32)
    rank_of = jnp.sum((jnp.cumsum(onehot, axis=1) - onehot) * onehot, axis=2).astype(jnp.int32)
    source = jnp.arange(devices, dtype=jnp.int32)[:, None]
    slot_index = ((id_table * devices + source) * MOST + rank_of).astype(jnp.int32)
    token_index = (source * TOK_DEV + jnp.arange(per_device, dtype=jnp.int32)[None, :] // TOPK).astype(jnp.int32)
    slot_total = EXPERTS * devices * MOST
    token_table = jnp.full((slot_total,), TOKENS, jnp.int32).at[slot_index.reshape(-1)].set(token_index.reshape(-1))
    weight_table = jnp.zeros((slot_total,), jnp.float32).at[slot_index.reshape(-1)].set(router_probs.reshape(-1).astype(jnp.float32))
    tok_pad = jnp.concatenate([tokens, jnp.zeros((1, D), jnp.bfloat16)], axis=0)
    grad_pad = jnp.concatenate([out_grad, jnp.zeros((1, D), jnp.bfloat16)], axis=0)

    def per_expert(inputs):
        table_e, prob_e, gate_w, up_w, down_w = inputs
        tok_slots = tok_pad[table_e]
        grad_slots = (prob_e[:, None] * grad_pad[table_e].astype(jnp.float32)).astype(jnp.bfloat16)
        return expert_pass(tok_slots, grad_slots, gate_w, up_w, down_w)

    outs_slots, back_slots, grad_gate, grad_up, grad_down = lax.map(
        per_expert,
        (token_table.reshape(EXPERTS, devices * MOST), weight_table.reshape(EXPERTS, devices * MOST), w_gate, w_up, w_down))
    out_flat = outs_slots.reshape(slot_total, D)
    back_flat = back_slots.reshape(slot_total, D)
    flat_slot = slot_index.reshape(TOKENS, TOPK)
    mixed = jnp.zeros((TOKENS, D), jnp.float32)
    input_grad = jnp.zeros((TOKENS, D), jnp.float32)
    grad_cols = []
    dy_float = out_grad.astype(jnp.float32)
    for k_index in range(TOPK):
        rows_k = out_flat[flat_slot[:, k_index]].astype(jnp.float32)
        mixed = mixed + router_probs[:, k_index:k_index + 1] * rows_k
        grad_cols.append(jnp.sum(dy_float * rows_k, axis=1))
        input_grad = input_grad + back_flat[flat_slot[:, k_index]].astype(jnp.float32)
    prob_grad = jnp.stack(grad_cols, axis=1)
    return (mixed.astype(jnp.bfloat16), input_grad.astype(jnp.bfloat16), prob_grad, grad_gate, grad_up, grad_down)
```

```python
import functools

import jax
import jax.numpy as jnp
from jax import lax
from jax.experimental import pallas as pl
from jax.experimental.pallas import tpu as pltpu
from jax.sharding import PartitionSpec as P


WIDE = 512
SLOTS = 4
LAG = 2

BF = jnp.bfloat16
F32 = jnp.float32
MESH = pl.DeviceIdType.MESH

IN_PARTS = (8, 8)
MIX_PARTS = (8, 8)
DX_PARTS = (8, 4, 4)

EARLY = True


def mm(a, b):
    return jnp.dot(a, b, preferred_element_type=F32)


def mm_nt(a, b):
    return lax.dot_general(a, b, (((1,), (1,)), ((), ())), preferred_element_type=F32)


def layer_kernel(
    n_dp, n_expert, block,
    meta_r, meta_c, tokens, out_grad, w_gate, w_up, w_down,
    mixed, input_grad, g_gate, g_up, g_down, pg_out,
    wg, wu, wd, tz, gz, stage, rows_t, rows_g, back,
    mr, mc, sel, sel_t,
    gate, up, dh, hid, dg, du, hid_t, dg_t, du_t,
    zstage, gstage, ostage, pgs, pgr, pzs, pzr,
    w_sem, tl_sem, gl_sem, m_send, m_recv,
    tz_send, tz_recv, gz_send, gz_recv, x_send,
    t_recv, g_recv, mx_recv, dx_recv, zr_send, zm_recv, zx_recv,
    gs_sem, os_sem, pg_send, pg_recv, pz_send, pz_recv, z_free, b_free,
):
    tok_rows = tz.shape[2]
    chunks = tz.shape[0]
    total = n_expert * block
    hidden_n = wg.shape[0]
    z_me = lax.axis_index("dp")
    e_me = lax.axis_index("expert")
    levels = n_expert.bit_length() - 1
    bits = [(e_me // (1 << j)) % 2 for j in range(levels)]

    def x_peer(m):
        out = 0
        for j in range(levels):
            bit = (1 - bits[j]) if (m >> j) & 1 else bits[j]
            out = out + bit * (1 << j)
        return {"expert": out}

    def z_peer(k):
        return {"dp": (z_me + k) % n_dp}

    far = sorted(range(1, n_expert), key=lambda m: -bin(m >> 1).count("1"))
    x_order = far

    def send(src, dst, s_sem, r_sem, peer):
        pltpu.make_async_remote_copy(
            src_ref=src, dst_ref=dst, send_sem=s_sem, recv_sem=r_sem,
            device_id=peer, device_id_type=MESH,
        ).start()

    def wait(ref, sem):
        pltpu.make_async_copy(ref, ref, sem).wait()

    def cols(i):
        return pl.ds(pl.multiple_of(i * WIDE, WIDE), WIDE)

    for i in range(chunks):
        pltpu.make_async_copy(tokens.at[:, cols(i)], tz.at[i, 0], tl_sem.at[i]).start()
    for i in range(chunks):
        pltpu.make_async_copy(out_grad.at[:, cols(i)], gz.at[i, 0], gl_sem.at[i]).start()
    for j, (w, v) in enumerate(((w_gate, wg), (w_up, wu), (w_down, wd))):
        pltpu.make_async_copy(w, v, w_sem.at[j]).start()

    barrier = pltpu.get_barrier_semaphore()
    for k in range(1, n_dp):
        pl.semaphore_signal(barrier, inc=1, device_id=z_peer(k), device_id_type=MESH)
    for m in range(1, n_expert):
        pl.semaphore_signal(barrier, inc=1, device_id=x_peer(m), device_id_type=MESH)
    pl.semaphore_wait(barrier, n_dp - 1 + n_expert - 1)

    for k in range(1, n_dp):
        send(meta_r, mr.at[k], m_send.at[0], m_recv.at[0], z_peer(k))
        send(meta_c, mc.at[k], m_send.at[1], m_recv.at[1], z_peer(k))

    @pl.loop(0, chunks)
    def _(i):
        wait(tz.at[i, 0], tl_sem.at[i])
        for k in range(1, n_dp):
            send(tz.at[i, 0], tz.at[i, k], tz_send.at[i], tz_recv.at[i], z_peer(k))

    others = pl.ds(1, n_dp - 1)
    rest = pl.ds(1, n_expert - 1)

    mr[0] = meta_r[...]
    mc[0] = meta_c[...]
    gate[...] = jnp.zeros_like(gate)
    up[...] = jnp.zeros_like(up)
    dh[...] = jnp.zeros_like(dh)
    pgs[...] = jnp.zeros_like(pgs)
    wait(mr.at[others], m_recv.at[0])
    wait(mc.at[others], m_recv.at[1])

    table = jnp.concatenate([mr[z] for z in range(n_dp)], axis=1)
    slot_r = lax.broadcasted_iota(jnp.int32, (block, n_dp * tok_rows), 0).astype(F32)

    def pick(hit, value):
        return jnp.where(hit, 1.0 if value is None else value, 0.0)

    def build_sel(weighted):
        for m in range(n_expert):
            y = None
            for k in range(2):
                hit = table[k : k + 1, :] == slot_r + float(m * block)
                v = pick(hit, table[2 + k : 3 + k, :] if weighted else None)
                y = v if y is None else y + v
            sel[m * block : (m + 1) * block, :] = y.astype(BF)

    slot_c = lax.broadcasted_iota(jnp.int32, (tok_rows, total), 1).astype(F32)

    def build_sel_t(weighted):
        for z in range(n_dp):
            part = mc[z]
            y = None
            for k in range(2):
                hit = part[:, k : k + 1] == slot_c
                v = pick(hit, part[:, 2 + k : 3 + k] if weighted else None)
                y = v if y is None else y + v
            sel_t[z * tok_rows : (z + 1) * tok_rows, :] = y.astype(BF)

    build_sel(False)

    def dispatch_unit(i, z_buf, s_mat, dst, r_sem):
        slot = lax.rem(i, SLOTS)
        whole = z_buf[i].reshape(n_dp * tok_rows, WIDE)
        for m in x_order + [0]:
            y = mm(s_mat[m * block : (m + 1) * block, :], whole).astype(BF)
            if m:
                stage[slot, m] = y
                send(stage.at[slot, m], dst.at[i, m], x_send.at[slot], r_sem.at[i], x_peer(m))
            else:
                dst[i, 0] = y

    @pl.loop(0, chunks)
    def _(i):
        @pl.when(i >= SLOTS)
        def _():
            slot = lax.rem(i, SLOTS)
            wait(stage.at[slot, rest], x_send.at[slot])

        wait(gz.at[i, 0], gl_sem.at[i])
        for k in range(1, n_dp):
            send(gz.at[i, 0], gz.at[i, k], gz_send.at[i], gz_recv.at[i], z_peer(k))
        wait(tz.at[i, others], tz_recv.at[i])
        dispatch_unit(i, tz, sel, rows_t, t_recv)

    build_sel(True)
    for j, (w, v) in enumerate(((w_gate, wg), (w_up, wu), (w_down, wd))):
        pltpu.make_async_copy(w, v, w_sem.at[j]).wait()

    pair = 2 * block

    @pl.loop(0, chunks)
    def _(i):
        slot = lax.rem(i, SLOTS)
        wait(stage.at[slot, rest], x_send.at[slot])
        wait(gz.at[i, others], gz_recv.at[i])
        dispatch_unit(i, gz, sel, rows_g, g_recv)
        wait(rows_t.at[i, rest], t_recv.at[i])
        for m in range(0, n_expert, 2):
            x = rows_t[i, m : m + 2].reshape(pair, WIDE)
            at = slice(m * block, (m + 2) * block)
            gate[at, :] += mm_nt(x, wg[:, cols(i)])
            up[at, :] += mm_nt(x, wu[:, cols(i)])

    @pl.loop(0, chunks)
    def _(i):
        wait(tz.at[i, others], tz_send.at[i])
        wait(gz.at[i, others], gz_send.at[i])

    for k in range(1, n_dp):
        pl.semaphore_signal(z_free, inc=1, device_id=z_peer(k), device_id_type=MESH)
    wait(mr.at[others], m_send.at[0])
    wait(mc.at[others], m_send.at[1])

    for j in range(total // 128):
        at = slice(j * 128, (j + 1) * 128)
        g = gate[at, :]
        h = g * jax.nn.sigmoid(g) * up[at, :]
        hid[at, :] = h.astype(BF)
        hid_t[:, at] = h.T.astype(BF)

    @pl.loop(0, chunks)
    def _(i):
        slot = lax.rem(i, SLOTS)
        wait(stage.at[slot, rest], x_send.at[slot])
        w = wd[:, cols(i)]
        for m in x_order + [0]:
            y = mm(hid[m * block : (m + 1) * block, :], w).astype(BF)
            if m:
                stage[slot, m] = y
                send(stage.at[slot, m], back.at[i, m], x_send.at[slot], mx_recv.at[i], x_peer(m))
            else:
                back[i, 0] = y
        wait(rows_g.at[i, rest], g_recv.at[i])
        for m in range(0, n_expert, 2):
            x = rows_g[i, m : m + 2].reshape(pair, WIDE)
            at = slice(m * block, (m + 2) * block)
            dh[at, :] += mm_nt(x, w)

    for j in range(total // 128):
        at = slice(j * 128, (j + 1) * 128)
        g = gate[at, :]
        s = jax.nn.sigmoid(g)
        d = dh[at, :]
        a = d * up[at, :] * s * (1.0 + g * (1.0 - s))
        b = d * (g * s)
        dg[at, :] = a.astype(BF)
        du[at, :] = b.astype(BF)
        dg_t[:, at] = a.T.astype(BF)
        du_t[:, at] = b.T.astype(BF)

    ones = jnp.ones((8, hidden_n), BF)

    def two(x):
        hi = x.astype(BF)
        return hi, (x - hi.astype(F32)).astype(BF)

    for m in x_order + [0]:
        at = slice(m * block, (m + 1) * block)
        hi, lo = two(hid[at, :].astype(F32) * dh[at, :])
        line = mm_nt(ones, hi) + mm_nt(ones, lo)
        if m:
            pgs[m, :, :block] = line
            send(pgs.at[m], pgr.at[m], pg_send, pg_recv, x_peer(m))
        else:
            pgs[0, :, :block] = line
    pgr[0] = pgs[0]

    build_sel_t(True)
    pl.semaphore_wait(z_free, n_dp - 1)

    def combine(i, s_mat, r_sem, keep, zr_recv):
        slot = lax.rem(i, 2)
        wait(back.at[i, rest], r_sem.at[i])
        rows = back[i].reshape(total, WIDE)
        for z in range(0, n_dp, 2):
            y = mm(s_mat[z * tok_rows : (z + 2) * tok_rows, :], rows).astype(BF)
            for k in (z, z + 1):
                piece = y[(k - z) * tok_rows : (k - z + 1) * tok_rows]
                if k:
                    zstage[slot, k] = piece
                    send(zstage.at[slot, k], keep.at[i, k], zr_send.at[slot], zr_recv.at[i], z_peer(n_dp - k))
                else:
                    keep[i, 0] = piece

    def finish(i, keep, zr_recv, out, first):
        slot = lax.rem(i, 2)
        wait(keep.at[i, others], zr_recv.at[i])
        y = keep[i, 0].astype(F32)
        for k in range(1, n_dp):
            y = y + keep[i, k].astype(F32)

        def drain():
            wait(ostage.at[slot], os_sem.at[slot])

        if first:
            pl.when(i >= 2)(drain)
        else:
            drain()
        ostage[slot] = y.astype(BF)
        pltpu.make_async_copy(ostage.at[slot], out.at[:, cols(i)], os_sem.at[slot]).start()

    @pl.loop(0, chunks)
    def _(i):
        two_slot = lax.rem(i, 2)

        @pl.when(i >= 2)
        def _():
            wait(zstage.at[two_slot, others], zr_send.at[two_slot])

        combine(i, sel_t, mx_recv, tz, zm_recv)
        for m in range(1, n_expert):
            pl.semaphore_signal(b_free.at[i], inc=1, device_id=x_peer(m), device_id_type=MESH)

        slot = lax.rem(i, SLOTS)
        wait(stage.at[slot, rest], x_send.at[slot])
        a, b = wg[:, cols(i)], wu[:, cols(i)]
        pl.semaphore_wait(b_free.at[i], n_expert - 1)
        for m in x_order + [0]:
            at = slice(m * block, (m + 1) * block)
            y = (mm(dg[at, :], a) + mm(du[at, :], b)).astype(BF)
            if m:
                stage[slot, m] = y
                send(stage.at[slot, m], back.at[i, m], x_send.at[slot], dx_recv.at[i], x_peer(m))
            else:
                back[i, 0] = y

        grads = ((hid_t, rows_g, g_down), (dg_t, rows_t, g_gate), (du_t, rows_t, g_up))
        for j, (left, right, out) in enumerate(grads):
            y = mm(left[...], right[i].reshape(total, WIDE)).astype(BF)

            @pl.when(i >= 1)
            def _():
                wait(gstage.at[j], gs_sem.at[j])

            gstage[j] = y
            pltpu.make_async_copy(gstage.at[j], out.at[:, cols(i)], gs_sem.at[j]).start()

        @pl.when(i >= LAG)
        def _():
            finish(i - LAG, tz, zm_recv, mixed, True)

    wait(pgr.at[rest], pg_recv)
    wait(pgs.at[rest], pg_send)
    found = [jnp.zeros((8, n_dp * tok_rows), F32), jnp.zeros((8, n_dp * tok_rows), F32)]
    for m in range(n_expert):
        hi, lo = two(pgr[m, :, :block])
        for k in range(2):
            hit = jnp.where(table[k : k + 1, :] == slot_r + float(m * block), 1.0, 0.0).astype(BF)
            found[k] = found[k] + (mm(hi, hit) + mm(lo, hit))
    for z in range(n_dp):
        at = slice(z * tok_rows, (z + 1) * tok_rows)
        pzs[z] = jnp.concatenate([found[0][0:4, at], found[1][0:4, at]], axis=0)
    for k in range(1, n_dp):
        send(pzs.at[k], pzr.at[k], pz_send, pz_recv, z_peer(n_dp - k))

    build_sel_t(False)
    for i in range(chunks - LAG, chunks):
        finish(i, tz, zm_recv, mixed, False)

    @pl.loop(0, chunks)
    def _(i):
        two_slot = lax.rem(i, 2)
        wait(zstage.at[two_slot, others], zr_send.at[two_slot])
        combine(i, sel_t, dx_recv, gz, zx_recv)

        @pl.when(i >= 1)
        def _():
            finish(i - 1, gz, zx_recv, input_grad, False)

    wait(pzr.at[others], pz_recv)
    wait(pzs.at[others], pz_send)
    line = pzs[0]
    for k in range(1, n_dp):
        line = line + pzr[k]
    pg_out[...] = line
    finish(chunks - 1, gz, zx_recv, input_grad, False)

    for s in range(SLOTS):
        wait(stage.at[s, rest], x_send.at[s])
    for s in range(2):
        wait(zstage.at[s, others], zr_send.at[s])
        wait(ostage.at[s], os_sem.at[s])
    for j in range(3):
        wait(gstage.at[j], gs_sem.at[j])


def by_kernel(tokens, expert_ids, router_probs, w_gate, w_up, w_down, out_grad):
    tok_rows, width = tokens.shape
    top = expert_ids.shape[1]
    n_expert = lax.axis_size("expert")
    n_dp = lax.axis_size("dp")
    depth = max(2, tok_rows * top * 9 // (8 * n_expert))
    block = n_dp * depth
    total = n_expert * block
    me = lax.axis_index("expert").astype(jnp.int32)
    dp_me = lax.axis_index("dp").astype(jnp.int32)
    hidden_n = w_gate.shape[1]
    chunks = width // WIDE

    flat = expert_ids.reshape(-1)
    onehot = (flat[:, None] == jnp.arange(n_expert, dtype=jnp.int32)[None, :]).astype(jnp.int32)
    rank = jnp.sum((jnp.cumsum(onehot, axis=0) - onehot) * onehot, axis=1).reshape(tok_rows, top)
    row = (expert_ids ^ me) * block + dp_me * depth + rank
    meta = jnp.concatenate([row.astype(F32), router_probs], axis=1)
    meta_c = jnp.pad(meta, ((0, 0), (0, 128 - 2 * top)))
    meta_r = jnp.pad(meta.T, ((0, 8 - 2 * top), (0, 0)))

    any_spec = pl.BlockSpec(memory_space=pl.ANY)
    vm_spec = pl.BlockSpec(memory_space=pltpu.VMEM)
    dma = pltpu.SemaphoreType.DMA
    tok_out = jax.ShapeDtypeStruct((tok_rows, width), BF)
    w_out = jax.ShapeDtypeStruct((hidden_n, width), BF)
    z_buf = pltpu.VMEM((chunks, n_dp, tok_rows, WIDE), BF)
    x_buf = pltpu.VMEM((chunks, n_expert, block, WIDE), BF)
    tall = pltpu.VMEM((total, n_dp * tok_rows), BF)
    broad = pltpu.VMEM((n_dp * tok_rows, total), BF)
    acc = pltpu.VMEM((total, hidden_n), F32)
    half = pltpu.VMEM((total, hidden_n), BF)
    half_t = pltpu.VMEM((hidden_n, total), BF)
    w_buf = pltpu.VMEM((hidden_n, width), BF)
    lanes = -(-block // 128) * 128
    scratch = (
        [w_buf] * 3
        + [z_buf] * 2
        + [pltpu.VMEM((SLOTS, n_expert, block, WIDE), BF)]
        + [x_buf] * 3
        + [pltpu.VMEM((n_dp, 8, tok_rows), F32), pltpu.VMEM((n_dp, tok_rows, 128), F32)]
        + [tall, broad]
        + [acc] * 3
        + [half] * 3
        + [half_t] * 3
        + [
            pltpu.VMEM((2, n_dp, tok_rows, WIDE), BF),
            pltpu.VMEM((3, hidden_n, WIDE), BF),
            pltpu.VMEM((2, tok_rows, WIDE), BF),
            pltpu.VMEM((n_expert, 8, lanes), F32),
            pltpu.VMEM((n_expert, 8, lanes), F32),
            pltpu.VMEM((n_dp, 8, tok_rows), F32),
            pltpu.VMEM((n_dp, 8, tok_rows), F32),
        ]
        + [dma((3,)), dma((chunks,)), dma((chunks,)), dma((2,)), dma((2,))]
        + [dma((chunks,))] * 4
        + [dma((SLOTS,))]
        + [dma((chunks,))] * 4
        + [dma((2,)), dma((chunks,)), dma((chunks,))]
        + [dma((3,)), dma((2,))]
        + [dma] * 4
        + [pltpu.SemaphoreType.REGULAR, pltpu.SemaphoreType.REGULAR((chunks,))]
    )
    mixed, input_grad, g_gate, g_up, g_down, pg = pl.pallas_call(
        functools.partial(layer_kernel, n_dp, n_expert, block),
        out_shape=[tok_out, tok_out, w_out, w_out, w_out, jax.ShapeDtypeStruct((8, tok_rows), F32)],
        in_specs=[vm_spec] * 2 + [any_spec] * 5,
        out_specs=[any_spec] * 5 + [vm_spec],
        scratch_shapes=scratch,
        compiler_params=pltpu.CompilerParams(
            collective_id=0, has_side_effects=True, vmem_limit_bytes=67000000
        ),
    )(meta_r, meta_c, tokens, out_grad, w_gate[0], w_up[0], w_down[0])
    own = jnp.stack([pg[0], pg[4]], axis=1)
    prob_grad = own / router_probs.astype(BF).astype(F32)
    return (mixed, input_grad, prob_grad, g_gate[None], g_up[None], g_down[None])


def dot(a, b, dims):
    return lax.dot_general(a, b, ((dims[:1], dims[1:]), ((), ())), preferred_element_type=F32)


def exchange(blocks):
    n = len(blocks)
    return [blocks[0]] + [
        lax.ppermute(blocks[m], "expert", [(i, i ^ m) for i in range(n)]) for m in range(1, n)
    ]


def by_collectives(tokens, expert_ids, router_probs, w_gate, w_up, w_down, out_grad):
    tok_rows, width = tokens.shape
    top = expert_ids.shape[1]
    n_expert = lax.axis_size("expert")
    n_dp = lax.axis_size("dp")
    depth = max(2, tok_rows * top * 9 // (8 * n_expert))
    block = n_dp * depth
    total = n_expert * block
    me = lax.axis_index("expert").astype(jnp.int32)
    w_gate, w_up, w_down = w_gate[0], w_up[0], w_down[0]

    flat = expert_ids.reshape(-1)
    onehot = (flat[:, None] == jnp.arange(n_expert, dtype=jnp.int32)[None, :]).astype(jnp.int32)
    rank = jnp.sum((jnp.cumsum(onehot, axis=0) - onehot) * onehot, axis=1).reshape(tok_rows, top)
    dp_me = lax.axis_index("dp").astype(jnp.int32)
    row = (expert_ids ^ me) * block + dp_me * depth + rank
    meta = jnp.concatenate([row.astype(F32), router_probs], axis=1)
    meta = lax.all_gather(meta, "dp", axis=0, tiled=True)
    rows_t = meta[:, :top].astype(jnp.int32).T
    probs_t = meta[:, top:].astype(BF).T

    def selector(values):
        r = lax.broadcasted_iota(jnp.int32, (total, 1), 0)
        out = jnp.zeros((total, rows_t.shape[1]), BF)
        for k in range(top):
            out = out + jnp.where(rows_t[k][None, :] == r, values[k], jnp.zeros((), BF))
        return out

    sel = selector([jnp.ones((), BF)] * top)
    selp = selector([probs_t[k][None, :] for k in range(top)])

    def columns(parts):
        edges = [0]
        for p in parts:
            edges.append(edges[-1] + p * width // 16)
        return [slice(lo, hi) for lo, hi in zip(edges[:-1], edges[1:])]

    def split(rows):
        return [rows[m * block : (m + 1) * block] for m in range(n_expert)]

    def gather(x):
        return [lax.all_gather(x[:, c], "dp", axis=0, tiled=True) for c in columns(IN_PARTS)]

    def dispatch(whole, s):
        return jnp.concatenate(exchange(split(dot(s, whole, (1, 0)).astype(BF))), axis=0)

    def contract(parts, w):
        out = None
        for part, c in zip(parts, columns(IN_PARTS)):
            term = dot(part, w[:, c], (1, 1))
            out = term if out is None else out + term
        return out

    def weight_grad(left, parts):
        return jnp.concatenate([dot(left, p, (0, 0)).astype(BF) for p in parts], axis=1)[None]

    def send_back(rows, s):
        back = jnp.concatenate(exchange(split(rows)), axis=0)
        mine = dot(s, back, (0, 0)).astype(BF)
        return lax.psum_scatter(mine, "dp", scatter_dimension=0, tiled=True)

    tok_parts = gather(tokens)
    og_parts = gather(out_grad)
    rows_in = [dispatch(x, sel) for x in tok_parts]
    grads_in = [dispatch(x, selp) for x in og_parts[:-1]]

    gate = contract(rows_in, w_gate)
    up = contract(rows_in, w_up)
    sig = jax.nn.sigmoid(gate)
    act = gate * sig
    hidden = (act * up).astype(BF)
    mixed_rows = [dot(hidden, w_down[:, c], (1, 0)).astype(BF) for c in columns(MIX_PARTS)]
    if EARLY:
        last, _ = lax.optimization_barrier((og_parts[-1], mixed_rows[0]))
    else:
        last = og_parts[-1]
    grads_in.append(dispatch(last, selp))
    mixed = jnp.concatenate([send_back(r, selp) for r in mixed_rows], axis=1)

    d_hidden = contract(grads_in, w_down)
    d_gate = (d_hidden * up * sig * (1.0 + gate * (1.0 - sig))).astype(BF)
    d_up = (d_hidden * act).astype(BF)
    d_both = jnp.concatenate([d_gate, d_up], axis=1)
    w_both = jnp.concatenate([w_gate, w_up], axis=0)
    input_grad = jnp.concatenate(
        [
            send_back(dot(d_both, w_both[:, c], (1, 0)).astype(BF), sel)
            for c in columns(DX_PARTS)
        ],
        axis=1,
    )

    scaled_pg = jnp.sum(hidden.astype(F32) * d_hidden, axis=1).reshape(n_expert, block)
    order = jnp.arange(n_expert, dtype=jnp.int32) ^ me
    pg = lax.all_to_all(scaled_pg[order], "expert", split_axis=0, concat_axis=0, tiled=True)
    pg = pg[order].reshape(-1)
    slots = lax.broadcasted_iota(jnp.int32, (total, 1), 0)
    pg = jnp.stack(
        [
            jnp.sum(jnp.where(rows_t[k][None, :] == slots, pg[:, None], 0.0), axis=0)
            for k in range(top)
        ],
        axis=1,
    ).reshape(n_dp, tok_rows, top)
    own = lax.dynamic_index_in_dim(pg, dp_me, 0, keepdims=False)
    for turn in range(1, n_dp):
        theirs = lax.dynamic_index_in_dim(pg, (dp_me + turn) % n_dp, 0, keepdims=False)
        own = own + lax.ppermute(theirs, "dp", [(i, (i + turn) % n_dp) for i in range(n_dp)])
    prob_grad = own / router_probs.astype(BF).astype(F32)

    grad_gate = weight_grad(d_gate, rows_in)
    grad_up = weight_grad(d_up, rows_in)
    grad_down = weight_grad(hidden, grads_in)
    return (mixed, input_grad, prob_grad, grad_gate, grad_up, grad_down)


def on_device(tokens, expert_ids, *rest):
    tok_rows, width = tokens.shape
    n_expert, n_dp = lax.axis_size("expert"), lax.axis_size("dp")
    depth = max(2, tok_rows * expert_ids.shape[1] * 9 // (8 * n_expert))
    fits = (n_dp * depth) % 16 == 0 and width % WIDE == 0 and n_dp % 2 == 0
    body = by_kernel if fits else by_collectives
    return body(tokens, expert_ids, *rest)


def solution(mesh):
    tok = P(("dp", "expert"), None)
    wt = P("expert", "dp", None)
    return jax.shard_map(
        on_device,
        mesh=mesh,
        in_specs=(tok, tok, tok, wt, wt, wt, tok),
        out_specs=(tok, tok, tok, wt, wt, wt),
        check_vma=False,
    )
```

```python
import functools

import jax
import jax.numpy as jnp
from jax import lax
from jax.experimental import pallas as pl
from jax.experimental.pallas import tpu as pltpu
from jax.sharding import PartitionSpec as P


WIDE = 256
SLOTS = 8
AHEAD = 4
BEHIND = 9

BF = jnp.bfloat16
F32 = jnp.float32
MESH = pl.DeviceIdType.MESH

IN_PARTS = (8, 8)
MIX_PARTS = (8, 8)
DX_PARTS = (8, 4, 4)

EARLY = True


def mm(a, b):
    return jnp.dot(a, b, preferred_element_type=F32)


def mm_nt(a, b):
    return lax.dot_general(a, b, (((1,), (1,)), ((), ())), preferred_element_type=F32)


def layer_kernel(
    n_dp, n_expert, block,
    meta_r, meta_c, tokens, out_grad, w_gate, w_up, w_down,
    mixed, input_grad, g_gate, g_up, g_down, pg_out,
    wg, wu, wd, tz, gz, stage, rows_t, rows_g, back,
    mr, mc, sel, sel_t,
    gate, up, dh, hid, dg, du, hid_t, dg_t, du_t,
    zstage, gstage, ostage, pgs, pgr, pzs, pzr,
    w_sem, tl_sem, gl_sem, m_send, m_recv,
    tz_send, tz_recv, gz_send, gz_recv, x_send,
    t_recv, g_recv, mx_recv, dx_recv, zr_send, zm_recv, zx_recv,
    gs_sem, os_sem, pg_send, pg_recv, pz_send, pz_recv, z_free, b_free,
):
    tok_rows = tz.shape[2]
    chunks = tz.shape[0]
    total = n_expert * block
    hidden_n = wg.shape[0]
    z_me = lax.axis_index("dp")
    e_me = lax.axis_index("expert")
    levels = n_expert.bit_length() - 1
    bits = [(e_me // (1 << j)) % 2 for j in range(levels)]

    def x_peer(m):
        out = 0
        for j in range(levels):
            bit = (1 - bits[j]) if (m >> j) & 1 else bits[j]
            out = out + bit * (1 << j)
        return {"expert": out}

    def z_peer(k):
        return {"dp": (z_me + k) % n_dp}

    far = sorted(range(1, n_expert), key=lambda m: -bin(m >> 1).count("1"))
    x_order = far

    def send(src, dst, s_sem, r_sem, peer):
        pltpu.make_async_remote_copy(
            src_ref=src, dst_ref=dst, send_sem=s_sem, recv_sem=r_sem,
            device_id=peer, device_id_type=MESH,
        ).start()

    def wait(ref, sem):
        pltpu.make_async_copy(ref, ref, sem).wait()

    def cols(i):
        return pl.ds(pl.multiple_of(i * WIDE, WIDE), WIDE)

    for i in range(chunks):
        pltpu.make_async_copy(tokens.at[:, cols(i)], tz.at[i, 0], tl_sem.at[i]).start()
    for i in range(chunks):
        pltpu.make_async_copy(out_grad.at[:, cols(i)], gz.at[i, 0], gl_sem.at[i]).start()
    for j, (w, v) in enumerate(((w_gate, wg), (w_up, wu), (w_down, wd))):
        pltpu.make_async_copy(w, v, w_sem.at[j]).start()

    barrier = pltpu.get_barrier_semaphore()
    for k in range(1, n_dp):
        pl.semaphore_signal(barrier, inc=1, device_id=z_peer(k), device_id_type=MESH)
    for m in range(1, n_expert):
        pl.semaphore_signal(barrier, inc=1, device_id=x_peer(m), device_id_type=MESH)
    pl.semaphore_wait(barrier, n_dp - 1 + n_expert - 1)

    for k in range(1, n_dp):
        send(meta_r, mr.at[k], m_send.at[0], m_recv.at[0], z_peer(k))
        send(meta_c, mc.at[k], m_send.at[1], m_recv.at[1], z_peer(k))

    def spread(i, z_buf, l_sem, s_sem, r_sem):
        wait(z_buf.at[i, 0], l_sem.at[i])
        for k in range(1, n_dp):
            send(z_buf.at[i, 0], z_buf.at[i, k], s_sem.at[i], r_sem.at[i], z_peer(k))

    def spread_tok(i):
        spread(i, tz, tl_sem, tz_send, tz_recv)

    def spread_grad(i):
        spread(i, gz, gl_sem, gz_send, gz_recv)

    for i in range(AHEAD):
        spread_tok(i)

    others = pl.ds(1, n_dp - 1)
    rest = pl.ds(1, n_expert - 1)

    mr[0] = meta_r[...]
    mc[0] = meta_c[...]
    gate[...] = jnp.zeros_like(gate)
    up[...] = jnp.zeros_like(up)
    dh[...] = jnp.zeros_like(dh)
    pgs[...] = jnp.zeros_like(pgs)
    wait(mr.at[others], m_recv.at[0])
    wait(mc.at[others], m_recv.at[1])

    table = jnp.concatenate([mr[z] for z in range(n_dp)], axis=1)
    slot_r = lax.broadcasted_iota(jnp.int32, (block, n_dp * tok_rows), 0).astype(F32)

    def pick(hit, value):
        return jnp.where(hit, 1.0 if value is None else value, 0.0)

    def build_sel(weighted):
        for m in range(n_expert):
            y = None
            for k in range(2):
                hit = table[k : k + 1, :] == slot_r + float(m * block)
                v = pick(hit, table[2 + k : 3 + k, :] if weighted else None)
                y = v if y is None else y + v
            sel[m * block : (m + 1) * block, :] = y.astype(BF)

    slot_c = lax.broadcasted_iota(jnp.int32, (tok_rows, total), 1).astype(F32)

    def build_sel_t(weighted):
        for z in range(n_dp):
            part = mc[z]
            y = None
            for k in range(2):
                hit = part[:, k : k + 1] == slot_c
                v = pick(hit, part[:, 2 + k : 3 + k] if weighted else None)
                y = v if y is None else y + v
            sel_t[z * tok_rows : (z + 1) * tok_rows, :] = y.astype(BF)

    build_sel(False)

    def dispatch_unit(i, z_buf, s_mat, dst, r_sem):
        slot = lax.rem(i, SLOTS)
        whole = z_buf[i].reshape(n_dp * tok_rows, WIDE)
        for m in x_order + [0]:
            y = mm(s_mat[m * block : (m + 1) * block, :], whole).astype(BF)
            if m:
                stage[slot, m] = y
                send(stage.at[slot, m], dst.at[i, m], x_send.at[slot], r_sem.at[i], x_peer(m))
            else:
                dst[i, 0] = y

    @pl.loop(0, chunks)
    def _(i):
        @pl.when(i >= SLOTS)
        def _():
            slot = lax.rem(i, SLOTS)
            wait(stage.at[slot, rest], x_send.at[slot])

        @pl.when(i < chunks - AHEAD)
        def _():
            spread_tok(i + AHEAD)

        @pl.when(i >= chunks - AHEAD)
        def _():
            spread_grad(i + AHEAD - chunks)

        wait(tz.at[i, others], tz_recv.at[i])
        dispatch_unit(i, tz, sel, rows_t, t_recv)

    build_sel(True)
    for j, (w, v) in enumerate(((w_gate, wg), (w_up, wu), (w_down, wd))):
        pltpu.make_async_copy(w, v, w_sem.at[j]).wait()

    pair = 2 * block

    @pl.loop(0, chunks)
    def _(i):
        slot = lax.rem(i, SLOTS)
        wait(stage.at[slot, rest], x_send.at[slot])

        @pl.when(i < chunks - AHEAD)
        def _():
            spread_grad(i + AHEAD)

        wait(gz.at[i, others], gz_recv.at[i])
        dispatch_unit(i, gz, sel, rows_g, g_recv)
        wait(rows_t.at[i, rest], t_recv.at[i])
        for m in range(0, n_expert, 2):
            x = rows_t[i, m : m + 2].reshape(pair, WIDE)
            at = slice(m * block, (m + 2) * block)
            gate[at, :] += mm_nt(x, wg[:, cols(i)])
            up[at, :] += mm_nt(x, wu[:, cols(i)])

    @pl.loop(0, chunks)
    def _(i):
        wait(tz.at[i, others], tz_send.at[i])
        wait(gz.at[i, others], gz_send.at[i])

    for k in range(1, n_dp):
        pl.semaphore_signal(z_free, inc=1, device_id=z_peer(k), device_id_type=MESH)
    wait(mr.at[others], m_send.at[0])
    wait(mc.at[others], m_send.at[1])

    for j in range(total // 128):
        at = slice(j * 128, (j + 1) * 128)
        g = gate[at, :]
        h = g * jax.nn.sigmoid(g) * up[at, :]
        hid[at, :] = h.astype(BF)
        hid_t[:, at] = h.T.astype(BF)

    def combine(i, r_sem, keep, zr_recv):
        slot = lax.rem(i, 2)
        wait(back.at[i, rest], r_sem.at[i])
        rows = back[i].reshape(total, WIDE)
        for z in range(0, n_dp, 2):
            y = mm(sel_t[z * tok_rows : (z + 2) * tok_rows, :], rows).astype(BF)
            for k in (z, z + 1):
                piece = y[(k - z) * tok_rows : (k - z + 1) * tok_rows]
                if k:
                    zstage[slot, k] = piece
                    send(zstage.at[slot, k], keep.at[i, k], zr_send.at[slot], zr_recv.at[i], z_peer(n_dp - k))
                else:
                    keep[i, 0] = piece

    def finish(i, keep, zr_recv, out, first):
        slot = lax.rem(i, 2)
        wait(keep.at[i, others], zr_recv.at[i])
        y = keep[i, 0].astype(F32)
        for k in range(1, n_dp):
            y = y + keep[i, k].astype(F32)

        def drain():
            wait(ostage.at[slot], os_sem.at[slot])

        if first:
            pl.when(i >= 2)(drain)
        else:
            drain()
        ostage[slot] = y.astype(BF)
        pltpu.make_async_copy(ostage.at[slot], out.at[:, cols(i)], os_sem.at[slot]).start()

    def step_m(j):
        @pl.when(j >= 2)
        def _():
            wait(zstage.at[lax.rem(j, 2), others], zr_send.at[lax.rem(j, 2)])

        combine(j, mx_recv, tz, zm_recv)
        for m in range(1, n_expert):
            pl.semaphore_signal(b_free.at[j], inc=1, device_id=x_peer(m), device_id_type=MESH)

        @pl.when(j >= 2)
        def _():
            finish(j - 2, tz, zm_recv, mixed, True)

    def step_x(j):
        wait(zstage.at[lax.rem(j, 2), others], zr_send.at[lax.rem(j, 2)])
        combine(j, dx_recv, gz, zx_recv)

        @pl.when(j < 2)
        def _():
            finish(j + chunks - 2, tz, zm_recv, mixed, False)

        @pl.when(j >= 2)
        def _():
            finish(j - 2, gz, zx_recv, input_grad, False)

    build_sel_t(True)
    pl.semaphore_wait(z_free, n_dp - 1)

    @pl.loop(0, chunks)
    def _(i):
        slot = lax.rem(i, SLOTS)
        wait(stage.at[slot, rest], x_send.at[slot])
        w = wd[:, cols(i)]
        for m in x_order + [0]:
            y = mm(hid[m * block : (m + 1) * block, :], w).astype(BF)
            if m:
                stage[slot, m] = y
                send(stage.at[slot, m], back.at[i, m], x_send.at[slot], mx_recv.at[i], x_peer(m))
            else:
                back[i, 0] = y
        wait(rows_g.at[i, rest], g_recv.at[i])
        for m in range(0, n_expert, 2):
            x = rows_g[i, m : m + 2].reshape(pair, WIDE)
            at = slice(m * block, (m + 2) * block)
            dh[at, :] += mm_nt(x, w)

        @pl.when(i >= BEHIND)
        def _():
            step_m(i - BEHIND)

    for j in range(total // 128):
        at = slice(j * 128, (j + 1) * 128)
        g = gate[at, :]
        s = jax.nn.sigmoid(g)
        d = dh[at, :]
        a = d * up[at, :] * s * (1.0 + g * (1.0 - s))
        b = d * (g * s)
        dg[at, :] = a.astype(BF)
        du[at, :] = b.astype(BF)
        dg_t[:, at] = a.T.astype(BF)
        du_t[:, at] = b.T.astype(BF)

    ones = jnp.ones((8, hidden_n), BF)

    def two(x):
        hi = x.astype(BF)
        return hi, (x - hi.astype(F32)).astype(BF)

    for m in x_order + [0]:
        at = slice(m * block, (m + 1) * block)
        hi, lo = two(hid[at, :].astype(F32) * dh[at, :])
        line = mm_nt(ones, hi) + mm_nt(ones, lo)
        if m:
            pgs[m, :, :block] = line
            send(pgs.at[m], pgr.at[m], pg_send, pg_recv, x_peer(m))
        else:
            pgs[0, :, :block] = line
    pgr[0] = pgs[0]


    def dx_unit(i):
        slot = lax.rem(i, SLOTS)
        wait(stage.at[slot, rest], x_send.at[slot])
        a, b = wg[:, cols(i)], wu[:, cols(i)]
        pl.semaphore_wait(b_free.at[i], n_expert - 1)
        for m in x_order + [0]:
            at = slice(m * block, (m + 1) * block)
            y = (mm(dg[at, :], a) + mm(du[at, :], b)).astype(BF)
            if m:
                stage[slot, m] = y
                send(stage.at[slot, m], back.at[i, m], x_send.at[slot], dx_recv.at[i], x_peer(m))
            else:
                back[i, 0] = y

        grads = ((hid_t, rows_g, g_down), (dg_t, rows_t, g_gate), (du_t, rows_t, g_up))
        for j, (left, right, out) in enumerate(grads):
            y = mm(left[...], right[i].reshape(total, WIDE)).astype(BF)

            @pl.when(i >= 1)
            def _():
                wait(gstage.at[j], gs_sem.at[j])

            gstage[j] = y
            pltpu.make_async_copy(gstage.at[j], out.at[:, cols(i)], gs_sem.at[j]).start()

    @pl.loop(0, BEHIND)
    def _(i):
        dx_unit(i)
        step_m(i + chunks - BEHIND)

    build_sel_t(False)

    @pl.loop(BEHIND, chunks)
    def _(i):
        dx_unit(i)
        step_x(i - BEHIND)

    wait(pgr.at[rest], pg_recv)
    wait(pgs.at[rest], pg_send)
    found = [jnp.zeros((8, n_dp * tok_rows), F32), jnp.zeros((8, n_dp * tok_rows), F32)]
    for m in range(n_expert):
        hi, lo = two(pgr[m, :, :block])
        for k in range(2):
            hit = jnp.where(table[k : k + 1, :] == slot_r + float(m * block), 1.0, 0.0).astype(BF)
            found[k] = found[k] + (mm(hi, hit) + mm(lo, hit))
    for z in range(n_dp):
        at = slice(z * tok_rows, (z + 1) * tok_rows)
        pzs[z] = jnp.concatenate([found[0][0:4, at], found[1][0:4, at]], axis=0)
    for k in range(1, n_dp):
        send(pzs.at[k], pzr.at[k], pz_send, pz_recv, z_peer(n_dp - k))

    @pl.loop(chunks - BEHIND, chunks)
    def _(i):
        step_x(i)

    wait(pzr.at[others], pz_recv)
    wait(pzs.at[others], pz_send)
    line = pzs[0]
    for k in range(1, n_dp):
        line = line + pzr[k]
    pg_out[...] = line
    finish(chunks - 2, gz, zx_recv, input_grad, False)
    finish(chunks - 1, gz, zx_recv, input_grad, False)

    for s in range(SLOTS):
        wait(stage.at[s, rest], x_send.at[s])
    for s in range(2):
        wait(zstage.at[s, others], zr_send.at[s])
        wait(ostage.at[s], os_sem.at[s])
    for j in range(3):
        wait(gstage.at[j], gs_sem.at[j])


def by_kernel(tokens, expert_ids, router_probs, w_gate, w_up, w_down, out_grad):
    tok_rows, width = tokens.shape
    top = expert_ids.shape[1]
    n_expert = lax.axis_size("expert")
    n_dp = lax.axis_size("dp")
    depth = max(2, tok_rows * top * 9 // (8 * n_expert))
    block = n_dp * depth
    total = n_expert * block
    me = lax.axis_index("expert").astype(jnp.int32)
    dp_me = lax.axis_index("dp").astype(jnp.int32)
    hidden_n = w_gate.shape[1]
    chunks = width // WIDE

    flat = expert_ids.reshape(-1)
    onehot = (flat[:, None] == jnp.arange(n_expert, dtype=jnp.int32)[None, :]).astype(jnp.int32)
    rank = jnp.sum((jnp.cumsum(onehot, axis=0) - onehot) * onehot, axis=1).reshape(tok_rows, top)
    row = (expert_ids ^ me) * block + dp_me * depth + rank
    meta = jnp.concatenate([row.astype(F32), router_probs], axis=1)
    meta_c = jnp.pad(meta, ((0, 0), (0, 128 - 2 * top)))
    meta_r = jnp.pad(meta.T, ((0, 8 - 2 * top), (0, 0)))

    any_spec = pl.BlockSpec(memory_space=pl.ANY)
    vm_spec = pl.BlockSpec(memory_space=pltpu.VMEM)
    dma = pltpu.SemaphoreType.DMA
    tok_out = jax.ShapeDtypeStruct((tok_rows, width), BF)
    w_out = jax.ShapeDtypeStruct((hidden_n, width), BF)
    z_buf = pltpu.VMEM((chunks, n_dp, tok_rows, WIDE), BF)
    x_buf = pltpu.VMEM((chunks, n_expert, block, WIDE), BF)
    tall = pltpu.VMEM((total, n_dp * tok_rows), BF)
    broad = pltpu.VMEM((n_dp * tok_rows, total), BF)
    acc = pltpu.VMEM((total, hidden_n), F32)
    half = pltpu.VMEM((total, hidden_n), BF)
    half_t = pltpu.VMEM((hidden_n, total), BF)
    w_buf = pltpu.VMEM((hidden_n, width), BF)
    lanes = -(-block // 128) * 128
    scratch = (
        [w_buf] * 3
        + [z_buf] * 2
        + [pltpu.VMEM((SLOTS, n_expert, block, WIDE), BF)]
        + [x_buf] * 3
        + [pltpu.VMEM((n_dp, 8, tok_rows), F32), pltpu.VMEM((n_dp, tok_rows, 128), F32)]
        + [tall, broad]
        + [acc] * 3
        + [half] * 3
        + [half_t] * 3
        + [
            pltpu.VMEM((2, n_dp, tok_rows, WIDE), BF),
            pltpu.VMEM((3, hidden_n, WIDE), BF),
            pltpu.VMEM((2, tok_rows, WIDE), BF),
            pltpu.VMEM((n_expert, 8, lanes), F32),
            pltpu.VMEM((n_expert, 8, lanes), F32),
            pltpu.VMEM((n_dp, 8, tok_rows), F32),
            pltpu.VMEM((n_dp, 8, tok_rows), F32),
        ]
        + [dma((3,)), dma((chunks,)), dma((chunks,)), dma((2,)), dma((2,))]
        + [dma((chunks,))] * 4
        + [dma((SLOTS,))]
        + [dma((chunks,))] * 4
        + [dma((2,)), dma((chunks,)), dma((chunks,))]
        + [dma((3,)), dma((2,))]
        + [dma] * 4
        + [pltpu.SemaphoreType.REGULAR, pltpu.SemaphoreType.REGULAR((chunks,))]
    )
    mixed, input_grad, g_gate, g_up, g_down, pg = pl.pallas_call(
        functools.partial(layer_kernel, n_dp, n_expert, block),
        out_shape=[tok_out, tok_out, w_out, w_out, w_out, jax.ShapeDtypeStruct((8, tok_rows), F32)],
        in_specs=[vm_spec] * 2 + [any_spec] * 5,
        out_specs=[any_spec] * 5 + [vm_spec],
        scratch_shapes=scratch,
        compiler_params=pltpu.CompilerParams(
            collective_id=0, has_side_effects=True, vmem_limit_bytes=67000000
        ),
    )(meta_r, meta_c, tokens, out_grad, w_gate[0], w_up[0], w_down[0])
    own = jnp.stack([pg[0], pg[4]], axis=1)
    prob_grad = own / router_probs.astype(BF).astype(F32)
    return (mixed, input_grad, prob_grad, g_gate[None], g_up[None], g_down[None])


def dot(a, b, dims):
    return lax.dot_general(a, b, ((dims[:1], dims[1:]), ((), ())), preferred_element_type=F32)


def exchange(blocks):
    n = len(blocks)
    return [blocks[0]] + [
        lax.ppermute(blocks[m], "expert", [(i, i ^ m) for i in range(n)]) for m in range(1, n)
    ]


def by_collectives(tokens, expert_ids, router_probs, w_gate, w_up, w_down, out_grad):
    tok_rows, width = tokens.shape
    top = expert_ids.shape[1]
    n_expert = lax.axis_size("expert")
    n_dp = lax.axis_size("dp")
    depth = max(2, tok_rows * top * 9 // (8 * n_expert))
    block = n_dp * depth
    total = n_expert * block
    me = lax.axis_index("expert").astype(jnp.int32)
    w_gate, w_up, w_down = w_gate[0], w_up[0], w_down[0]

    flat = expert_ids.reshape(-1)
    onehot = (flat[:, None] == jnp.arange(n_expert, dtype=jnp.int32)[None, :]).astype(jnp.int32)
    rank = jnp.sum((jnp.cumsum(onehot, axis=0) - onehot) * onehot, axis=1).reshape(tok_rows, top)
    dp_me = lax.axis_index("dp").astype(jnp.int32)
    row = (expert_ids ^ me) * block + dp_me * depth + rank
    meta = jnp.concatenate([row.astype(F32), router_probs], axis=1)
    meta = lax.all_gather(meta, "dp", axis=0, tiled=True)
    rows_t = meta[:, :top].astype(jnp.int32).T
    probs_t = meta[:, top:].astype(BF).T

    def selector(values):
        r = lax.broadcasted_iota(jnp.int32, (total, 1), 0)
        out = jnp.zeros((total, rows_t.shape[1]), BF)
        for k in range(top):
            out = out + jnp.where(rows_t[k][None, :] == r, values[k], jnp.zeros((), BF))
        return out

    sel = selector([jnp.ones((), BF)] * top)
    selp = selector([probs_t[k][None, :] for k in range(top)])

    def columns(parts):
        edges = [0]
        for p in parts:
            edges.append(edges[-1] + p * width // 16)
        return [slice(lo, hi) for lo, hi in zip(edges[:-1], edges[1:])]

    def split(rows):
        return [rows[m * block : (m + 1) * block] for m in range(n_expert)]

    def gather(x):
        return [lax.all_gather(x[:, c], "dp", axis=0, tiled=True) for c in columns(IN_PARTS)]

    def dispatch(whole, s):
        return jnp.concatenate(exchange(split(dot(s, whole, (1, 0)).astype(BF))), axis=0)

    def contract(parts, w):
        out = None
        for part, c in zip(parts, columns(IN_PARTS)):
            term = dot(part, w[:, c], (1, 1))
            out = term if out is None else out + term
        return out

    def weight_grad(left, parts):
        return jnp.concatenate([dot(left, p, (0, 0)).astype(BF) for p in parts], axis=1)[None]

    def send_back(rows, s):
        back = jnp.concatenate(exchange(split(rows)), axis=0)
        mine = dot(s, back, (0, 0)).astype(BF)
        return lax.psum_scatter(mine, "dp", scatter_dimension=0, tiled=True)

    tok_parts = gather(tokens)
    og_parts = gather(out_grad)
    rows_in = [dispatch(x, sel) for x in tok_parts]
    grads_in = [dispatch(x, selp) for x in og_parts[:-1]]

    gate = contract(rows_in, w_gate)
    up = contract(rows_in, w_up)
    sig = jax.nn.sigmoid(gate)
    act = gate * sig
    hidden = (act * up).astype(BF)
    mixed_rows = [dot(hidden, w_down[:, c], (1, 0)).astype(BF) for c in columns(MIX_PARTS)]
    if EARLY:
        last, _ = lax.optimization_barrier((og_parts[-1], mixed_rows[0]))
    else:
        last = og_parts[-1]
    grads_in.append(dispatch(last, selp))
    mixed = jnp.concatenate([send_back(r, selp) for r in mixed_rows], axis=1)

    d_hidden = contract(grads_in, w_down)
    d_gate = (d_hidden * up * sig * (1.0 + gate * (1.0 - sig))).astype(BF)
    d_up = (d_hidden * act).astype(BF)
    d_both = jnp.concatenate([d_gate, d_up], axis=1)
    w_both = jnp.concatenate([w_gate, w_up], axis=0)
    input_grad = jnp.concatenate(
        [
            send_back(dot(d_both, w_both[:, c], (1, 0)).astype(BF), sel)
            for c in columns(DX_PARTS)
        ],
        axis=1,
    )

    scaled_pg = jnp.sum(hidden.astype(F32) * d_hidden, axis=1).reshape(n_expert, block)
    order = jnp.arange(n_expert, dtype=jnp.int32) ^ me
    pg = lax.all_to_all(scaled_pg[order], "expert", split_axis=0, concat_axis=0, tiled=True)
    pg = pg[order].reshape(-1)
    slots = lax.broadcasted_iota(jnp.int32, (total, 1), 0)
    pg = jnp.stack(
        [
            jnp.sum(jnp.where(rows_t[k][None, :] == slots, pg[:, None], 0.0), axis=0)
            for k in range(top)
        ],
        axis=1,
    ).reshape(n_dp, tok_rows, top)
    own = lax.dynamic_index_in_dim(pg, dp_me, 0, keepdims=False)
    for turn in range(1, n_dp):
        theirs = lax.dynamic_index_in_dim(pg, (dp_me + turn) % n_dp, 0, keepdims=False)
        own = own + lax.ppermute(theirs, "dp", [(i, (i + turn) % n_dp) for i in range(n_dp)])
    prob_grad = own / router_probs.astype(BF).astype(F32)

    grad_gate = weight_grad(d_gate, rows_in)
    grad_up = weight_grad(d_up, rows_in)
    grad_down = weight_grad(hidden, grads_in)
    return (mixed, input_grad, prob_grad, grad_gate, grad_up, grad_down)


def on_device(tokens, expert_ids, *rest):
    tok_rows, width = tokens.shape
    n_expert, n_dp = lax.axis_size("expert"), lax.axis_size("dp")
    depth = max(2, tok_rows * expert_ids.shape[1] * 9 // (8 * n_expert))
    fits = (n_dp * depth) % 16 == 0 and width % WIDE == 0 and n_dp % 2 == 0
    body = by_kernel if fits else by_collectives
    return body(tokens, expert_ids, *rest)


def solution(mesh):
    tok = P(("dp", "expert"), None)
    wt = P("expert", "dp", None)
    return jax.shard_map(
        on_device,
        mesh=mesh,
        in_specs=(tok, tok, tok, wt, wt, wt, tok),
        out_specs=(tok, tok, tok, wt, wt, wt),
        check_vma=False,
    )
```

```python
import functools

import jax
import jax.numpy as jnp
from jax import lax
from jax.experimental import pallas as pl
from jax.experimental.pallas import tpu as pltpu
from jax.sharding import PartitionSpec as P


WIDE = 256
SLOTS = 8
AHEAD = 3
BEHIND = 9

BF = jnp.bfloat16
F32 = jnp.float32
MESH = pl.DeviceIdType.MESH

IN_PARTS = (8, 8)
MIX_PARTS = (8, 8)
DX_PARTS = (8, 4, 4)

EARLY = True


def mm(a, b):
    return jnp.dot(a, b, preferred_element_type=F32)


def mm_nt(a, b):
    return lax.dot_general(a, b, (((1,), (1,)), ((), ())), preferred_element_type=F32)


def layer_kernel(
    n_dp, n_expert, depth,
    ids, probs, tokens, out_grad, w_gate, w_up, w_down,
    mixed, input_grad, g_gate, g_up, g_down, pg_out,
    wg, wu, wd, tz, gz, stage, rows_t, rows_g, back,
    mr, mc, sel, sel_t,
    gate, up, dh, hid, dg, du, hid_t, dg_t, du_t,
    zstage, gstage, ostage, pgs, pgr, pzs, pzr,
    w_sem, tl_sem, gl_sem, m_send, m_recv,
    tz_send, tz_recv, gz_send, gz_recv, x_send,
    t_recv, g_recv, mx_recv, dx_recv, zr_send, zm_recv, zx_recv,
    gs_sem, os_sem, pg_send, pg_recv, pz_send, pz_recv, z_free, b_free,
):
    tok_rows = tz.shape[2]
    chunks = tz.shape[0]
    block = n_dp * depth
    total = n_expert * block
    hidden_n = wg.shape[0]
    z_me = lax.axis_index("dp")
    e_me = lax.axis_index("expert")
    levels = n_expert.bit_length() - 1
    bits = [(e_me // (1 << j)) % 2 for j in range(levels)]

    def x_peer(m):
        out = 0
        for j in range(levels):
            bit = (1 - bits[j]) if (m >> j) & 1 else bits[j]
            out = out + bit * (1 << j)
        return {"expert": out}

    def z_peer(k):
        return {"dp": (z_me + k) % n_dp}

    far = sorted(range(1, n_expert), key=lambda m: -bin(m >> 1).count("1"))
    x_order = far

    def send(src, dst, s_sem, r_sem, peer):
        pltpu.make_async_remote_copy(
            src_ref=src, dst_ref=dst, send_sem=s_sem, recv_sem=r_sem,
            device_id=peer, device_id_type=MESH,
        ).start()

    def wait(ref, sem):
        pltpu.make_async_copy(ref, ref, sem).wait()

    def cols(i):
        return pl.ds(pl.multiple_of(i * WIDE, WIDE), WIDE)

    for i in range(chunks):
        pltpu.make_async_copy(tokens.at[:, cols(i)], tz.at[i, 0], tl_sem.at[i]).start()
    for i in range(chunks):
        pltpu.make_async_copy(out_grad.at[:, cols(i)], gz.at[i, 0], gl_sem.at[i]).start()
    for j, (w, v) in enumerate(((w_gate, wg), (w_up, wu), (w_down, wd))):
        pltpu.make_async_copy(w, v, w_sem.at[j]).start()

    barrier = pltpu.get_barrier_semaphore()
    for k in range(1, n_dp):
        pl.semaphore_signal(barrier, inc=1, device_id=z_peer(k), device_id_type=MESH)
    for m in range(1, n_expert):
        pl.semaphore_signal(barrier, inc=1, device_id=x_peer(m), device_id_type=MESH)

    who = lax.broadcasted_iota(jnp.int32, (n_expert, tok_rows), 0)
    names = [jnp.where(who == ids[k : k + 1, :], 1.0, 0.0) for k in range(2)]
    before = lax.broadcasted_iota(jnp.int32, (tok_rows, tok_rows), 0) < lax.broadcasted_iota(
        jnp.int32, (tok_rows, tok_rows), 1
    )
    earlier = mm((names[0] + names[1]).astype(BF), jnp.where(before, 1.0, 0.0).astype(BF))
    mr[0] = jnp.zeros_like(mr[0])
    for k in range(2):
        rank = jnp.sum(earlier * names[k], axis=0, keepdims=True)
        base = jnp.bitwise_xor(ids[k : k + 1, :], e_me) * block + z_me * depth
        mr[0, k : k + 1, :] = base.astype(F32) + rank
        mr[0, 2 + k : 3 + k, :] = probs[k : k + 1, :]
    mc[0] = jnp.concatenate([mr[0], jnp.zeros((128 - 8, tok_rows), F32)], axis=0).T

    pl.semaphore_wait(barrier, n_dp - 1 + n_expert - 1)

    for k in range(1, n_dp):
        send(mr.at[0], mr.at[k], m_send.at[0], m_recv.at[0], z_peer(k))
        send(mc.at[0], mc.at[k], m_send.at[1], m_recv.at[1], z_peer(k))

    def spread(i, z_buf, l_sem, s_sem, r_sem):
        wait(z_buf.at[i, 0], l_sem.at[i])
        for k in range(1, n_dp):
            send(z_buf.at[i, 0], z_buf.at[i, k], s_sem.at[i], r_sem.at[i], z_peer(k))

    def spread_tok(i):
        spread(i, tz, tl_sem, tz_send, tz_recv)

    def spread_grad(i):
        spread(i, gz, gl_sem, gz_send, gz_recv)

    for i in range(AHEAD):
        spread_tok(i)

    others = pl.ds(1, n_dp - 1)
    rest = pl.ds(1, n_expert - 1)

    gate[...] = jnp.zeros_like(gate)
    up[...] = jnp.zeros_like(up)
    dh[...] = jnp.zeros_like(dh)
    pgs[...] = jnp.zeros_like(pgs)
    wait(mr.at[others], m_recv.at[0])
    wait(mc.at[others], m_recv.at[1])

    table = jnp.concatenate([mr[z] for z in range(n_dp)], axis=1)
    slot_r = lax.broadcasted_iota(jnp.int32, (block, n_dp * tok_rows), 0).astype(F32)

    def pick(hit, value):
        return jnp.where(hit, 1.0 if value is None else value, 0.0)

    def build_sel(weighted):
        for m in range(n_expert):
            y = None
            for k in range(2):
                hit = table[k : k + 1, :] == slot_r + float(m * block)
                v = pick(hit, table[2 + k : 3 + k, :] if weighted else None)
                y = v if y is None else y + v
            sel[m * block : (m + 1) * block, :] = y.astype(BF)

    slot_c = lax.broadcasted_iota(jnp.int32, (tok_rows, total), 1).astype(F32)

    def build_sel_t(weighted):
        for z in range(n_dp):
            part = mc[z]
            y = None
            for k in range(2):
                hit = part[:, k : k + 1] == slot_c
                v = pick(hit, part[:, 2 + k : 3 + k] if weighted else None)
                y = v if y is None else y + v
            sel_t[z * tok_rows : (z + 1) * tok_rows, :] = y.astype(BF)

    build_sel(False)

    def dispatch_unit(i, z_buf, s_mat, dst, r_sem):
        slot = lax.rem(i, SLOTS)
        whole = z_buf[i].reshape(n_dp * tok_rows, WIDE)
        for m in x_order + [0]:
            y = mm(s_mat[m * block : (m + 1) * block, :], whole).astype(BF)
            if m:
                stage[slot, m] = y
                send(stage.at[slot, m], dst.at[i, m], x_send.at[slot], r_sem.at[i], x_peer(m))
            else:
                dst[i, 0] = y

    @pl.loop(0, chunks)
    def _(i):
        @pl.when(i >= SLOTS)
        def _():
            slot = lax.rem(i, SLOTS)
            wait(stage.at[slot, rest], x_send.at[slot])

        @pl.when(i < chunks - AHEAD)
        def _():
            spread_tok(i + AHEAD)

        @pl.when(i >= chunks - AHEAD)
        def _():
            spread_grad(i + AHEAD - chunks)

        wait(tz.at[i, others], tz_recv.at[i])
        dispatch_unit(i, tz, sel, rows_t, t_recv)

    build_sel(True)
    for j, (w, v) in enumerate(((w_gate, wg), (w_up, wu), (w_down, wd))):
        pltpu.make_async_copy(w, v, w_sem.at[j]).wait()

    pair = 2 * block

    @pl.loop(0, chunks)
    def _(i):
        slot = lax.rem(i, SLOTS)
        wait(stage.at[slot, rest], x_send.at[slot])

        @pl.when(i < chunks - AHEAD)
        def _():
            spread_grad(i + AHEAD)

        wait(gz.at[i, others], gz_recv.at[i])
        dispatch_unit(i, gz, sel, rows_g, g_recv)
        wait(rows_t.at[i, rest], t_recv.at[i])
        for m in range(0, n_expert, 2):
            x = rows_t[i, m : m + 2].reshape(pair, WIDE)
            at = slice(m * block, (m + 2) * block)
            gate[at, :] += mm_nt(x, wg[:, cols(i)])
            up[at, :] += mm_nt(x, wu[:, cols(i)])

    @pl.loop(0, chunks)
    def _(i):
        wait(tz.at[i, others], tz_send.at[i])
        wait(gz.at[i, others], gz_send.at[i])

    for k in range(1, n_dp):
        pl.semaphore_signal(z_free, inc=1, device_id=z_peer(k), device_id_type=MESH)
    wait(mr.at[others], m_send.at[0])
    wait(mc.at[others], m_send.at[1])

    for j in range(total // 128):
        at = slice(j * 128, (j + 1) * 128)
        g = gate[at, :]
        h = g * jax.nn.sigmoid(g) * up[at, :]
        hid[at, :] = h.astype(BF)
        hid_t[:, at] = h.T.astype(BF)

    def combine(i, r_sem, keep, zr_recv):
        slot = lax.rem(i, 2)
        wait(back.at[i, rest], r_sem.at[i])
        rows = back[i].reshape(total, WIDE)
        for z in range(0, n_dp, 2):
            y = mm(sel_t[z * tok_rows : (z + 2) * tok_rows, :], rows).astype(BF)
            for k in (z, z + 1):
                piece = y[(k - z) * tok_rows : (k - z + 1) * tok_rows]
                if k:
                    zstage[slot, k] = piece
                    send(zstage.at[slot, k], keep.at[i, k], zr_send.at[slot], zr_recv.at[i], z_peer(n_dp - k))
                else:
                    keep[i, 0] = piece

    def finish(i, keep, zr_recv, out, first):
        slot = lax.rem(i, 2)
        wait(keep.at[i, others], zr_recv.at[i])
        y = keep[i, 0].astype(F32)
        for k in range(1, n_dp):
            y = y + keep[i, k].astype(F32)

        def drain():
            wait(ostage.at[slot], os_sem.at[slot])

        if first:
            pl.when(i >= 2)(drain)
        else:
            drain()
        ostage[slot] = y.astype(BF)
        pltpu.make_async_copy(ostage.at[slot], out.at[:, cols(i)], os_sem.at[slot]).start()

    def step_m(j):
        @pl.when(j >= 2)
        def _():
            wait(zstage.at[lax.rem(j, 2), others], zr_send.at[lax.rem(j, 2)])

        combine(j, mx_recv, tz, zm_recv)
        for m in range(1, n_expert):
            pl.semaphore_signal(b_free.at[j], inc=1, device_id=x_peer(m), device_id_type=MESH)

        @pl.when(j >= 2)
        def _():
            finish(j - 2, tz, zm_recv, mixed, True)

    def step_x(j):
        wait(zstage.at[lax.rem(j, 2), others], zr_send.at[lax.rem(j, 2)])
        combine(j, dx_recv, gz, zx_recv)

        @pl.when(j < 2)
        def _():
            finish(j + chunks - 2, tz, zm_recv, mixed, False)

        @pl.when(j >= 2)
        def _():
            finish(j - 2, gz, zx_recv, input_grad, False)

    build_sel_t(True)
    pl.semaphore_wait(z_free, n_dp - 1)

    @pl.loop(0, chunks)
    def _(i):
        slot = lax.rem(i, SLOTS)
        wait(stage.at[slot, rest], x_send.at[slot])
        w = wd[:, cols(i)]
        for m in x_order + [0]:
            y = mm(hid[m * block : (m + 1) * block, :], w).astype(BF)
            if m:
                stage[slot, m] = y
                send(stage.at[slot, m], back.at[i, m], x_send.at[slot], mx_recv.at[i], x_peer(m))
            else:
                back[i, 0] = y
        wait(rows_g.at[i, rest], g_recv.at[i])
        for m in range(0, n_expert, 2):
            x = rows_g[i, m : m + 2].reshape(pair, WIDE)
            at = slice(m * block, (m + 2) * block)
            dh[at, :] += mm_nt(x, w)

        @pl.when(i >= BEHIND)
        def _():
            step_m(i - BEHIND)

    for j in range(total // 128):
        at = slice(j * 128, (j + 1) * 128)
        g = gate[at, :]
        s = jax.nn.sigmoid(g)
        d = dh[at, :]
        a = d * up[at, :] * s * (1.0 + g * (1.0 - s))
        b = d * (g * s)
        dg[at, :] = a.astype(BF)
        du[at, :] = b.astype(BF)
        dg_t[:, at] = a.T.astype(BF)
        du_t[:, at] = b.T.astype(BF)

    ones = jnp.ones((8, hidden_n), BF)

    def two(x):
        hi = x.astype(BF)
        return hi, (x - hi.astype(F32)).astype(BF)

    for m in x_order + [0]:
        at = slice(m * block, (m + 1) * block)
        hi, lo = two(hid[at, :].astype(F32) * dh[at, :])
        line = mm_nt(ones, hi) + mm_nt(ones, lo)
        if m:
            pgs[m, :, :block] = line
            send(pgs.at[m], pgr.at[m], pg_send, pg_recv, x_peer(m))
        else:
            pgs[0, :, :block] = line
    pgr[0] = pgs[0]


    def dx_unit(i):
        slot = lax.rem(i, SLOTS)
        wait(stage.at[slot, rest], x_send.at[slot])
        a, b = wg[:, cols(i)], wu[:, cols(i)]
        pl.semaphore_wait(b_free.at[i], n_expert - 1)
        for m in x_order + [0]:
            at = slice(m * block, (m + 1) * block)
            y = (mm(dg[at, :], a) + mm(du[at, :], b)).astype(BF)
            if m:
                stage[slot, m] = y
                send(stage.at[slot, m], back.at[i, m], x_send.at[slot], dx_recv.at[i], x_peer(m))
            else:
                back[i, 0] = y

        grads = ((hid_t, rows_g, g_down), (dg_t, rows_t, g_gate), (du_t, rows_t, g_up))
        for j, (left, right, out) in enumerate(grads):
            y = mm(left[...], right[i].reshape(total, WIDE)).astype(BF)

            @pl.when(i >= 1)
            def _():
                wait(gstage.at[j], gs_sem.at[j])

            gstage[j] = y
            pltpu.make_async_copy(gstage.at[j], out.at[:, cols(i)], gs_sem.at[j]).start()

    @pl.loop(0, BEHIND)
    def _(i):
        dx_unit(i)
        step_m(i + chunks - BEHIND)

    build_sel_t(False)

    @pl.loop(BEHIND, chunks)
    def _(i):
        dx_unit(i)
        step_x(i - BEHIND)

    wait(pgr.at[rest], pg_recv)
    wait(pgs.at[rest], pg_send)
    found = [jnp.zeros((8, n_dp * tok_rows), F32), jnp.zeros((8, n_dp * tok_rows), F32)]
    for m in range(n_expert):
        hi, lo = two(pgr[m, :, :block])
        for k in range(2):
            hit = jnp.where(table[k : k + 1, :] == slot_r + float(m * block), 1.0, 0.0).astype(BF)
            found[k] = found[k] + (mm(hi, hit) + mm(lo, hit))
    for z in range(n_dp):
        at = slice(z * tok_rows, (z + 1) * tok_rows)
        pzs[z] = jnp.concatenate([found[0][0:4, at], found[1][0:4, at]], axis=0)
    for k in range(1, n_dp):
        send(pzs.at[k], pzr.at[k], pz_send, pz_recv, z_peer(n_dp - k))

    @pl.loop(chunks - BEHIND, chunks)
    def _(i):
        step_x(i)

    wait(pzr.at[others], pz_recv)
    wait(pzs.at[others], pz_send)
    line = pzs[0]
    for k in range(1, n_dp):
        line = line + pzr[k]
    for k in range(2):
        pg_out[k : k + 1, :] = line[4 * k : 4 * k + 1, :] / probs[k : k + 1, :].astype(BF).astype(F32)
    finish(chunks - 2, gz, zx_recv, input_grad, False)
    finish(chunks - 1, gz, zx_recv, input_grad, False)

    for s in range(SLOTS):
        wait(stage.at[s, rest], x_send.at[s])
    for s in range(2):
        wait(zstage.at[s, others], zr_send.at[s])
        wait(ostage.at[s], os_sem.at[s])
    for j in range(3):
        wait(gstage.at[j], gs_sem.at[j])


def by_kernel(tokens, expert_ids, router_probs, w_gate, w_up, w_down, out_grad):
    tok_rows, width = tokens.shape
    top = expert_ids.shape[1]
    n_expert = lax.axis_size("expert")
    n_dp = lax.axis_size("dp")
    depth = max(2, tok_rows * top * 9 // (8 * n_expert))
    block = n_dp * depth
    total = n_expert * block
    hidden_n = w_gate.shape[1]
    chunks = width // WIDE

    any_spec = pl.BlockSpec(memory_space=pl.ANY)
    vm_spec = pl.BlockSpec(memory_space=pltpu.VMEM)
    dma = pltpu.SemaphoreType.DMA
    tok_out = jax.ShapeDtypeStruct((tok_rows, width), BF)
    w_out = jax.ShapeDtypeStruct((hidden_n, width), BF)
    z_buf = pltpu.VMEM((chunks, n_dp, tok_rows, WIDE), BF)
    x_buf = pltpu.VMEM((chunks, n_expert, block, WIDE), BF)
    tall = pltpu.VMEM((total, n_dp * tok_rows), BF)
    broad = pltpu.VMEM((n_dp * tok_rows, total), BF)
    acc = pltpu.VMEM((total, hidden_n), F32)
    half = pltpu.VMEM((total, hidden_n), BF)
    half_t = pltpu.VMEM((hidden_n, total), BF)
    w_buf = pltpu.VMEM((hidden_n, width), BF)
    lanes = -(-block // 128) * 128
    scratch = (
        [w_buf] * 3
        + [z_buf] * 2
        + [pltpu.VMEM((SLOTS, n_expert, block, WIDE), BF)]
        + [x_buf] * 3
        + [pltpu.VMEM((n_dp, 8, tok_rows), F32), pltpu.VMEM((n_dp, tok_rows, 128), F32)]
        + [tall, broad]
        + [acc] * 3
        + [half] * 3
        + [half_t] * 3
        + [
            pltpu.VMEM((2, n_dp, tok_rows, WIDE), BF),
            pltpu.VMEM((3, hidden_n, WIDE), BF),
            pltpu.VMEM((2, tok_rows, WIDE), BF),
            pltpu.VMEM((n_expert, 8, lanes), F32),
            pltpu.VMEM((n_expert, 8, lanes), F32),
            pltpu.VMEM((n_dp, 8, tok_rows), F32),
            pltpu.VMEM((n_dp, 8, tok_rows), F32),
        ]
        + [dma((3,)), dma((chunks,)), dma((chunks,)), dma((2,)), dma((2,))]
        + [dma((chunks,))] * 4
        + [dma((SLOTS,))]
        + [dma((chunks,))] * 4
        + [dma((2,)), dma((chunks,)), dma((chunks,))]
        + [dma((3,)), dma((2,))]
        + [dma] * 4
        + [pltpu.SemaphoreType.REGULAR, pltpu.SemaphoreType.REGULAR((chunks,))]
    )
    mixed, input_grad, g_gate, g_up, g_down, pg = pl.pallas_call(
        functools.partial(layer_kernel, n_dp, n_expert, depth),
        out_shape=[tok_out, tok_out, w_out, w_out, w_out, jax.ShapeDtypeStruct((top, tok_rows), F32)],
        in_specs=[vm_spec] * 2 + [any_spec] * 5,
        out_specs=[any_spec] * 5 + [vm_spec],
        scratch_shapes=scratch,
        compiler_params=pltpu.CompilerParams(
            collective_id=0, has_side_effects=True, vmem_limit_bytes=67000000
        ),
    )(expert_ids.T, router_probs.T, tokens, out_grad, w_gate[0], w_up[0], w_down[0])
    return (mixed, input_grad, pg.T, g_gate[None], g_up[None], g_down[None])


def dot(a, b, dims):
    return lax.dot_general(a, b, ((dims[:1], dims[1:]), ((), ())), preferred_element_type=F32)


def exchange(blocks):
    n = len(blocks)
    return [blocks[0]] + [
        lax.ppermute(blocks[m], "expert", [(i, i ^ m) for i in range(n)]) for m in range(1, n)
    ]


def by_collectives(tokens, expert_ids, router_probs, w_gate, w_up, w_down, out_grad):
    tok_rows, width = tokens.shape
    top = expert_ids.shape[1]
    n_expert = lax.axis_size("expert")
    n_dp = lax.axis_size("dp")
    depth = max(2, tok_rows * top * 9 // (8 * n_expert))
    block = n_dp * depth
    total = n_expert * block
    me = lax.axis_index("expert").astype(jnp.int32)
    w_gate, w_up, w_down = w_gate[0], w_up[0], w_down[0]

    flat = expert_ids.reshape(-1)
    onehot = (flat[:, None] == jnp.arange(n_expert, dtype=jnp.int32)[None, :]).astype(jnp.int32)
    rank = jnp.sum((jnp.cumsum(onehot, axis=0) - onehot) * onehot, axis=1).reshape(tok_rows, top)
    dp_me = lax.axis_index("dp").astype(jnp.int32)
    row = (expert_ids ^ me) * block + dp_me * depth + rank
    meta = jnp.concatenate([row.astype(F32), router_probs], axis=1)
    meta = lax.all_gather(meta, "dp", axis=0, tiled=True)
    rows_t = meta[:, :top].astype(jnp.int32).T
    probs_t = meta[:, top:].astype(BF).T

    def selector(values):
        r = lax.broadcasted_iota(jnp.int32, (total, 1), 0)
        out = jnp.zeros((total, rows_t.shape[1]), BF)
        for k in range(top):
            out = out + jnp.where(rows_t[k][None, :] == r, values[k], jnp.zeros((), BF))
        return out

    sel = selector([jnp.ones((), BF)] * top)
    selp = selector([probs_t[k][None, :] for k in range(top)])

    def columns(parts):
        edges = [0]
        for p in parts:
            edges.append(edges[-1] + p * width // 16)
        return [slice(lo, hi) for lo, hi in zip(edges[:-1], edges[1:])]

    def split(rows):
        return [rows[m * block : (m + 1) * block] for m in range(n_expert)]

    def gather(x):
        return [lax.all_gather(x[:, c], "dp", axis=0, tiled=True) for c in columns(IN_PARTS)]

    def dispatch(whole, s):
        return jnp.concatenate(exchange(split(dot(s, whole, (1, 0)).astype(BF))), axis=0)

    def contract(parts, w):
        out = None
        for part, c in zip(parts, columns(IN_PARTS)):
            term = dot(part, w[:, c], (1, 1))
            out = term if out is None else out + term
        return out

    def weight_grad(left, parts):
        return jnp.concatenate([dot(left, p, (0, 0)).astype(BF) for p in parts], axis=1)[None]

    def send_back(rows, s):
        back = jnp.concatenate(exchange(split(rows)), axis=0)
        mine = dot(s, back, (0, 0)).astype(BF)
        return lax.psum_scatter(mine, "dp", scatter_dimension=0, tiled=True)

    tok_parts = gather(tokens)
    og_parts = gather(out_grad)
    rows_in = [dispatch(x, sel) for x in tok_parts]
    grads_in = [dispatch(x, selp) for x in og_parts[:-1]]

    gate = contract(rows_in, w_gate)
    up = contract(rows_in, w_up)
    sig = jax.nn.sigmoid(gate)
    act = gate * sig
    hidden = (act * up).astype(BF)
    mixed_rows = [dot(hidden, w_down[:, c], (1, 0)).astype(BF) for c in columns(MIX_PARTS)]
    if EARLY:
        last, _ = lax.optimization_barrier((og_parts[-1], mixed_rows[0]))
    else:
        last = og_parts[-1]
    grads_in.append(dispatch(last, selp))
    mixed = jnp.concatenate([send_back(r, selp) for r in mixed_rows], axis=1)

    d_hidden = contract(grads_in, w_down)
    d_gate = (d_hidden * up * sig * (1.0 + gate * (1.0 - sig))).astype(BF)
    d_up = (d_hidden * act).astype(BF)
    d_both = jnp.concatenate([d_gate, d_up], axis=1)
    w_both = jnp.concatenate([w_gate, w_up], axis=0)
    input_grad = jnp.concatenate(
        [
            send_back(dot(d_both, w_both[:, c], (1, 0)).astype(BF), sel)
            for c in columns(DX_PARTS)
        ],
        axis=1,
    )

    scaled_pg = jnp.sum(hidden.astype(F32) * d_hidden, axis=1).reshape(n_expert, block)
    order = jnp.arange(n_expert, dtype=jnp.int32) ^ me
    pg = lax.all_to_all(scaled_pg[order], "expert", split_axis=0, concat_axis=0, tiled=True)
    pg = pg[order].reshape(-1)
    slots = lax.broadcasted_iota(jnp.int32, (total, 1), 0)
    pg = jnp.stack(
        [
            jnp.sum(jnp.where(rows_t[k][None, :] == slots, pg[:, None], 0.0), axis=0)
            for k in range(top)
        ],
        axis=1,
    ).reshape(n_dp, tok_rows, top)
    own = lax.dynamic_index_in_dim(pg, dp_me, 0, keepdims=False)
    for turn in range(1, n_dp):
        theirs = lax.dynamic_index_in_dim(pg, (dp_me + turn) % n_dp, 0, keepdims=False)
        own = own + lax.ppermute(theirs, "dp", [(i, (i + turn) % n_dp) for i in range(n_dp)])
    prob_grad = own / router_probs.astype(BF).astype(F32)

    grad_gate = weight_grad(d_gate, rows_in)
    grad_up = weight_grad(d_up, rows_in)
    grad_down = weight_grad(hidden, grads_in)
    return (mixed, input_grad, prob_grad, grad_gate, grad_up, grad_down)


def on_device(tokens, expert_ids, *rest):
    tok_rows, width = tokens.shape
    n_expert, n_dp = lax.axis_size("expert"), lax.axis_size("dp")
    depth = max(2, tok_rows * expert_ids.shape[1] * 9 // (8 * n_expert))
    fits = (n_dp * depth) % 16 == 0 and width % WIDE == 0 and n_dp % 2 == 0
    body = by_kernel if fits else by_collectives
    return body(tokens, expert_ids, *rest)


def solution(mesh):
    tok = P(("dp", "expert"), None)
    wt = P("expert", "dp", None)
    return jax.shard_map(
        on_device,
        mesh=mesh,
        in_specs=(tok, tok, tok, wt, wt, wt, tok),
        out_specs=(tok, tok, tok, wt, wt, wt),
        check_vma=False,
    )
```
